32 devices in a mesh: rep: 8 (over z, x), batch: 4 (over y, core).
Axes of the slice: x: 2, y: 2, z: 4, core: 2. Of those that a mesh axis runs over, the one named last changes fastest.
Arguments:
- embed: bfloat16 [4096, 1024], P(('rep', 'batch')), may hold values from -9 to 9
- actions: int32 [4096, 5], P(('rep', 'batch')), may hold values from 0 to 17
- rewards: float32 [4096, 5], P(('rep', 'batch')), may hold values from -1 to 1
- ends: int32 [4096, 5], P(('rep', 'batch')), may hold values 0 or 1
- behaviour: float32 [4096, 5, 18], P(('rep', 'batch')), may hold values from -5 to 5
- w_hidden: bfloat16 [1024, 1024], replicated, may hold values from -0.1875 to 0.1875
- w_action: bfloat16 [18, 1024], replicated, may hold values from -3 to 3
- w_heads: bfloat16 [1024, 36], replicated, may hold values from -0.1875 to 0.1875
Outputs:
- grad_hidden: float32 [1024, 1024], replicated
- grad_action: float32 [18, 1024], replicated
- grad_heads: float32 [1024, 36], replicated
- targets: float32 [4096, 5], P(('rep', 'batch'))
The draws below stay inside these ranges and needn't reach their ends.
All inputs are finite; a program needn't handle non-finite values. No bound on the sum of `ends` on one device may be relied on, other than what follows from the above.
Results may differ from the reference program's by a relative error of at most 0.0057.
Values sent between devices are 32-bit elements; how exact they have to be, the bound alone decides.
A program may use at most 64 MiB of HBM per device.

```python
import jax
import jax.numpy as jnp
from jax import lax

HID = 1024
ACTIONS = 18
STEPS = 5
B_DEV = 128
TOTAL = 4096
N_REP = 8
N_BATCH = 4
DEVICES = 32


def draw_embed(key, part):
    key_here = jax.random.fold_in(key, 7)
    row_ids = jnp.arange(TOTAL, dtype=jnp.int32)
    lane = row_ids // B_DEV % N_BATCH
    frac = lane.astype(jnp.float32) / float(max(N_BATCH - 1, 1))
    base = jnp.clip(jax.random.normal(key_here, (TOTAL, HID), jnp.float32), -6.0, 6.0)
    scale = 0.5 * jnp.power(3.0, frac)
    return (base * scale[:, None]).astype(jnp.bfloat16)


def place_ends(result, key, low, high):
    longest = result.shape.index(max(result.shape))
    spots = []
    for shift in (0, 1):
        where = [jax.random.randint(jax.random.fold_in(key, axis), (), 0, length) for axis, length in enumerate(result.shape)]
        where[longest] = (where[longest] + shift) % result.shape[longest]
        spots.append(tuple(where))
    return result.at[spots[0]].set(low).at[spots[1]].set(high)


def block_scale(own_key, extent, shards, smallest, high):
    loudness = 1.0
    for dim, parts in shards:
        steps = jax.random.uniform(jax.random.fold_in(jax.random.fold_in(own_key, 6), dim), (parts,), jnp.float32, smallest / len(shards), high / len(shards))
        loudness = loudness * jnp.repeat(jnp.exp(steps), extent[dim] // parts).reshape((-1,) + (1,) * (len(extent) - 1 - dim))
    return loudness


def noise(rng, dims, scale, reach, pieces=(), kind=jnp.bfloat16):
    result = jax.random.normal(rng, dims, jnp.float32) * scale
    if len(pieces) > 0:
        result = block_scale(rng, dims, pieces, -0.22, 0.18) * result
    return jnp.clip(result, min=-reach, max=reach).astype(kind)


def setup_inputs(seed: int = 0) -> dict:
    streams_of = jax.random.split(jax.random.key(seed), 9)
    return {
        "embed": draw_embed(jax.random.fold_in(streams_of[8], 71), 0),
        "actions": place_ends(jax.random.randint(streams_of[1], (TOTAL, STEPS), 0, ACTIONS), jax.random.fold_in(streams_of[1], 1), 0, ACTIONS - 1).astype(jnp.int32),
        "rewards": jnp.clip(jax.random.uniform(streams_of[2], (TOTAL, STEPS), jnp.float32, -1.0, 1.0) * block_scale(streams_of[2], (TOTAL, STEPS), ((0, 32),), -0.4, 0.0), -1.0, 1.0),
        "ends": place_ends((jax.random.randint(streams_of[3], (TOTAL, STEPS), 0, 8) < 1).astype(jnp.int32), jax.random.fold_in(streams_of[3], 1), 0, 1),
        "behaviour": noise(streams_of[4], (TOTAL, STEPS, ACTIONS), 1.0, 5.0, ((0, 32),), jnp.float32),
        "w_hidden": noise(streams_of[5], (HID, HID), HID ** -0.5, 0.1875),
        "w_action": noise(streams_of[6], (ACTIONS, HID), 0.5, 3.0),
        "w_heads": noise(streams_of[7], (HID, 2 * ACTIONS), HID ** -0.5, 0.1875),
    }


DISCOUNT = 0.997
TRACE_LAMBDA = 0.95
EPSILON = 1e-06

def unroll(emb_block, act_block, w_hidden, w_action, w_heads):
    act_count = w_action.shape[0]
    unroll_len = act_block.shape[1]
    onehot = (act_block[:, :, None] == jnp.arange(act_count, dtype=jnp.int32)[None, None, :]).astype(jnp.bfloat16)
    hidden_state = emb_block.astype(jnp.float32)
    rounded = []
    squashed = []
    head_out = []
    for step in range(unroll_len):
        state_bf16 = hidden_state.astype(jnp.bfloat16)
        rounded.append(state_bf16)
        head_out.append(jnp.dot(state_bf16, w_heads, preferred_element_type=jnp.float32))
        preact = jnp.dot(state_bf16, w_hidden, preferred_element_type=jnp.float32)
        preact = preact + jnp.dot(onehot[:, step], w_action, preferred_element_type=jnp.float32)
        squash = jnp.tanh(preact)
        squashed.append(squash)
        hidden_state = hidden_state + squash
    state_bf16 = hidden_state.astype(jnp.bfloat16)
    head_out.append(jnp.dot(state_bf16, w_heads, preferred_element_type=jnp.float32))
    return (jnp.stack(head_out), rounded, squashed, onehot)

def estimates(head_out, actions, rewards, ends, behaviour):
    act_count = behaviour.shape[-1]
    unroll_len = actions.shape[1]
    logits = head_out[:, :, :act_count]
    qvalues = head_out[:, :, act_count:]
    exp_logits = jnp.exp(logits)
    policy = exp_logits / lax.optimization_barrier(jnp.sum(exp_logits, axis=-1, keepdims=True))
    values = lax.optimization_barrier(jnp.sum(policy * qvalues, axis=-1))
    onehot_f = (jnp.transpose(actions)[:, :, None] == jnp.arange(act_count, dtype=jnp.int32)[None, None, :]).astype(jnp.float32)
    logpol = logits[:unroll_len] - jnp.log(lax.optimization_barrier(jnp.sum(exp_logits[:unroll_len], axis=-1, keepdims=True)))
    behave = jnp.transpose(behaviour, (1, 0, 2))
    behave_log = behave - jnp.log(lax.optimization_barrier(jnp.sum(jnp.exp(behave), axis=-1, keepdims=True)))
    ratios = jnp.exp(lax.optimization_barrier(jnp.sum(onehot_f * (logpol - behave_log), axis=-1)))
    clipped = jnp.minimum(1.0, ratios)
    not_ended = 1.0 - jnp.transpose(ends).astype(jnp.float32)
    td_error = jnp.transpose(rewards) + DISCOUNT * not_ended * values[1:] - values[:unroll_len]
    carried = jnp.zeros_like(values[0])
    collected = []
    for step in range(unroll_len - 1, -1, -1):
        carried = clipped[step] * td_error[step] + DISCOUNT * TRACE_LAMBDA * not_ended[step] * clipped[step] * carried
        collected.append(carried)
    collected = jnp.stack(collected[::-1])
    targets = values[:unroll_len] + collected
    advantage = qvalues[:unroll_len] - values[:unroll_len, :, None]
    return (policy[:unroll_len], onehot_f, targets, advantage)

def objective(head_out, onehot_f, targets, cmpo_policy, taken_weight, norm_scale):
    act_count = onehot_f.shape[-1]
    unroll_len = onehot_f.shape[0]
    logits = head_out[:unroll_len, :, :act_count]
    qvalues = head_out[:unroll_len, :, act_count:]
    logpol = logits - jnp.log(lax.optimization_barrier(jnp.sum(jnp.exp(logits), axis=-1, keepdims=True)))
    q_taken = lax.optimization_barrier(jnp.sum(onehot_f * qvalues, axis=-1))
    value_term = 0.5 * (q_taken - targets) ** 2
    policy_term = -taken_weight * lax.optimization_barrier(jnp.sum(onehot_f * logpol, axis=-1))
    regular = -lax.optimization_barrier(jnp.sum(cmpo_policy * logpol, axis=-1))
    return jnp.sum(value_term + policy_term + regular) * norm_scale

def backward(cotangent, rounded, squashed, onehot, w_hidden, w_heads):
    unroll_len = len(squashed)
    hid = w_hidden.shape[0]
    grad_state = jnp.zeros(squashed[0].shape, jnp.float32)
    grad_hidden = jnp.zeros((hid, hid), jnp.float32)
    grad_action = jnp.zeros((hid, onehot.shape[-1]), jnp.float32)
    grad_heads = jnp.zeros(w_heads.shape, jnp.float32)
    for step in range(unroll_len - 1, -1, -1):
        grad_pre = (grad_state * (1.0 - squashed[step] * squashed[step])).astype(jnp.bfloat16)
        head_cot = cotangent[step].astype(jnp.bfloat16)
        grad_hidden = grad_hidden + jnp.dot(rounded[step].T, grad_pre, preferred_element_type=jnp.float32)
        grad_action = grad_action + jnp.dot(grad_pre.T, onehot[:, step], preferred_element_type=jnp.float32)
        grad_heads = grad_heads + jnp.dot(rounded[step].T, head_cot, preferred_element_type=jnp.float32)
        grad_state = grad_state + jnp.dot(grad_pre, w_hidden.T, preferred_element_type=jnp.float32)
        grad_state = grad_state + jnp.dot(head_cot, w_heads.T, preferred_element_type=jnp.float32)
    return (grad_hidden, grad_action, grad_heads)

def reference(embed, actions, rewards, ends, behaviour, w_hidden, w_action, w_heads):
    emb_blocks = embed.reshape(DEVICES, B_DEV, HID)
    act_blocks = actions.reshape(DEVICES, B_DEV, STEPS)

    def heads_of(inputs):
        return unroll(inputs[0], inputs[1], w_hidden, w_action, w_heads)[0]
    head_out = lax.map(heads_of, (emb_blocks, act_blocks))
    head_out = jnp.transpose(head_out, (1, 0, 2, 3)).reshape(STEPS + 1, TOTAL, 2 * ACTIONS)
    policy, onehot_f, targets, advantage = estimates(head_out, actions, rewards, ends, behaviour)
    grouped = advantage.reshape(STEPS, N_REP, N_BATCH * B_DEV, ACTIONS)
    spread = lax.optimization_barrier(jnp.sum(grouped * grouped, axis=(0, 2, 3)))
    spread_scale = jnp.sqrt(spread / (N_BATCH * B_DEV * STEPS * ACTIONS) + EPSILON)
    scale_rows = jnp.repeat(spread_scale, N_BATCH * B_DEV, total_repeat_length=TOTAL)
    weights = jnp.exp(jnp.clip(advantage / scale_rows[None, :, None], -1.0, 1.0))
    norm_mass = lax.optimization_barrier(jnp.sum(policy * weights, axis=-1))
    mass_sum = lax.optimization_barrier(jnp.sum(norm_mass.reshape(STEPS, N_REP, N_BATCH * B_DEV), axis=(0, 2)))
    mean_mass = mass_sum / (N_BATCH * B_DEV * STEPS)
    mass_rows = jnp.repeat(mean_mass, N_BATCH * B_DEV, total_repeat_length=TOTAL)
    cmpo_policy = policy * weights / norm_mass[:, :, None]
    taken_weight = lax.optimization_barrier(jnp.sum(onehot_f * weights, axis=-1)) / mass_rows[None, :]
    cotangent = jax.grad(objective)(head_out, onehot_f, targets, cmpo_policy, taken_weight, 1.0 / (TOTAL * STEPS))
    cot_blocks = jnp.transpose(cotangent.reshape(STEPS + 1, DEVICES, B_DEV, 2 * ACTIONS), (1, 0, 2, 3))

    def accumulate(sums_acc, inputs):
        _, rounded, squashed, onehot = unroll(inputs[0], inputs[1], w_hidden, w_action, w_heads)
        partial_value = backward(inputs[2], rounded, squashed, onehot, w_hidden, w_heads)
        return ((sums_acc[0] + partial_value[0], sums_acc[1] + partial_value[1], sums_acc[2] + partial_value[2]), None)
    zero_sums = (jnp.zeros((HID, HID), jnp.float32), jnp.zeros((HID, ACTIONS), jnp.float32), jnp.zeros((HID, 2 * ACTIONS), jnp.float32))
    summed, _ = lax.scan(accumulate, zero_sums, (emb_blocks, act_blocks, cot_blocks))
    return (summed[0], summed[1].T, summed[2], targets.T)
```

```python
import functools

import jax
import jax.numpy as jnp
from jax import lax
from jax.experimental import pallas as pl
from jax.experimental.pallas import tpu as pltpu
from jax.sharding import PartitionSpec as P

DISCOUNT = 0.997
TRACE_LAMBDA = 0.95
EPSILON = 1e-06
MESH = pl.DeviceIdType.MESH
COLORS = 4
F32 = jnp.float32
BF16 = jnp.bfloat16


def place_of(device):
    coords = getattr(device, "coords", None)
    if coords is None:
        return None
    return tuple(coords) + (getattr(device, "core_on_chip", 0),)


def topology(mesh):
    devices = mesh.devices
    origin = place_of(devices[(0,) * devices.ndim])
    dims = {}
    for position, axis in enumerate(mesh.axis_names):
        stride = 1
        while stride < devices.shape[position]:
            index = [0] * devices.ndim
            index[position] = stride
            here = place_of(devices[tuple(index)])
            if here is None or origin is None:
                last = position == devices.ndim - 1 and stride == 1
                key, far = ((3,) if last else (0, position, stride)), 1
            else:
                moved = [d for d in range(len(here)) if here[d] != origin[d]]
                key, far = (moved[0],), abs(here[moved[0]] - origin[moved[0]])
            dims.setdefault(key, []).append((far, (axis, stride)))
            stride *= 2
    core = dims.pop((3,))[0][1]
    chips = [[bit for _, bit in sorted(dims[key])] for key in sorted(dims)]
    return core, chips


def color_orders(chips):
    near = [bits[0] for bits in chips]
    rest = [bit for bits in chips for bit in bits[1:]]
    if len(near) == 3:
        perms = ((0, 1, 2), (1, 0, 2), (2, 0, 1), (1, 2, 0))
    else:
        n = len(near)
        perms = [[(i + j) % n for j in range(n)] for i in range(COLORS)]
    return [[near[i] for i in perm] + rest for perm in perms]


def subsets(bits):
    out = [()]
    for bit in bits:
        out = out + [s + (bit,) for s in out]
    return [s for s in out if s]


def bit_value(bit):
    axis, stride = bit
    return lax.rem(lax.axis_index(axis) // stride, 2)


def partner(bits):
    where = {}
    for axis, stride in bits:
        at = lax.axis_index(axis)
        moved = where.get(axis, at)
        where[axis] = moved + (1 - 2 * lax.rem(at // stride, 2)) * stride
    return where


def dot(a, b, ca, cb):
    return lax.dot_general(a, b, (((ca,), (cb,)), ((), ())), preferred_element_type=F32)


def main_kernel(
    cfg, embed_in, act_in, rew_in, ends_in, beh_in, wh_in, wa_in, wht_in,
    out, tgt, embed, act, rew, ends, beh, wh, wa, wht, in_sem,
    grads, rcore, rbuf, s_all, x_all, s_t, deriv, h_ref, r_ref, whp32, whp, wap, onehot, g32, g_all,
    ssend, srecv,
    ss_sem, sr_sem, c1s, c1r, rss, rsr, ags, agr, c2s, c2r,
):
    core_bit, orders, group, everyone, devices, group_count = cfg
    rows, hid = embed.shape
    steps = act.shape[0]
    acts = wa.shape[0]
    apad = wap.shape[0]
    qrow = whp.shape[0] // 2
    total_rows = grads.shape[1]
    width = grads.shape[2]
    stages = len(orders[0])

    loads = []
    for i, (source, target) in enumerate((
        (embed_in, embed), (act_in, act), (rew_in, rew), (ends_in, ends),
        (beh_in, beh), (wa_in, wa), (wht_in, wht), (wh_in, wh),
    )):
        loads.append(pltpu.make_async_copy(source, target, in_sem.at[i]))
        loads[-1].start()

    barrier = pltpu.get_barrier_semaphore()
    for bits in everyone:
        pl.semaphore_signal(barrier, inc=1, device_id=partner(bits), device_id_type=MESH)

    for load in loads[:-1]:
        load.wait()

    whp32[...] = jnp.zeros_like(whp32)
    whp32[0:acts, :] = wht[0:acts, :].astype(F32)
    whp32[qrow : qrow + acts, :] = wht[acts : 2 * acts, :].astype(F32)
    whp[...] = whp32[...].astype(BF16)
    whp32[...] = jnp.zeros_like(whp32)
    whp32[0:acts, :] = wa[...].astype(F32)
    wap[...] = whp32[0:apad, :].astype(BF16)
    rows_iota = lax.broadcasted_iota(jnp.int32, (apad, rows), 0)
    for k in range(steps):
        hot = rows_iota == act[k : k + 1, :]
        onehot[:, k * rows : (k + 1) * rows] = jnp.where(hot, 1.0, 0.0).astype(BF16)

    loads[-1].wait()
    heads = []
    h_ref[...] = embed[...].astype(F32)
    for k in range(steps + 1):
        s = h_ref[...].astype(BF16)
        if k < steps:
            s_all[k * rows : (k + 1) * rows, :] = s
            pre = dot(s, wh[...], 1, 0) + dot(onehot[:, k * rows : (k + 1) * rows], wap[...], 0, 0)
            t = jnp.tanh(pre)
            h_ref[...] = h_ref[...] + t
            if k < steps - 1:
                deriv[k] = 1.0 - t * t
                s_t[:, k * rows : (k + 1) * rows] = s.T
        heads.append(dot(whp[...], s, 1, 1))

    logits = [o[0:acts] for o in heads]
    qs = [o[qrow : qrow + acts] for o in heads]
    pis, values, logpis, hots, clipped = [], [], [], [], []
    small_iota = lax.broadcasted_iota(jnp.int32, (acts, rows), 0)
    for k in range(steps + 1):
        e = jnp.exp(logits[k])
        z = jnp.sum(e, axis=0, keepdims=True)
        pi = e / z
        pis.append(pi)
        values.append(jnp.sum(pi * qs[k], axis=0, keepdims=True))
        if k < steps:
            logpi = logits[k] - jnp.log(z)
            b = beh[k]
            mu = b - jnp.log(jnp.sum(jnp.exp(b), axis=0, keepdims=True))
            hot = jnp.where(small_iota == act[k : k + 1, :], 1.0, 0.0)
            hots.append(hot)
            ratio = jnp.exp(jnp.sum(hot * (logpi - mu), axis=0, keepdims=True))
            clipped.append(jnp.minimum(1.0, ratio))
    carried = jnp.zeros_like(values[0])
    targets = [None] * steps
    for k in range(steps - 1, -1, -1):
        live = 1.0 - ends[k : k + 1, :].astype(F32)
        delta = rew[k : k + 1, :] + DISCOUNT * live * values[k + 1] - values[k]
        carried = clipped[k] * delta + DISCOUNT * TRACE_LAMBDA * live * clipped[k] * carried
        targets[k] = values[k] + carried
        tgt[k : k + 1, :] = targets[k]
    advs = [qs[k] - values[k] for k in range(steps)]

    pl.semaphore_wait(barrier, len(everyone))

    def group_sum(slot, value):
        ssend[slot] = jnp.broadcast_to(value, ssend.shape[1:])
        copies = [
            pltpu.make_async_remote_copy(
                src_ref=ssend.at[slot], dst_ref=srecv.at[slot, i],
                send_sem=ss_sem.at[slot, i], recv_sem=sr_sem.at[slot, i],
                device_id=partner(bits), device_id_type=MESH,
            )
            for i, bits in enumerate(group)
        ]
        for copy in copies:
            copy.start()

        def finish():
            for copy in copies:
                copy.wait()
            total = ssend[slot]
            for i in range(len(group)):
                total = total + srecv[slot, i]
            return total[0:1, 0:1]

        return finish

    def total_of(parts):
        acc = parts[0]
        for part in parts[1:]:
            acc = acc + part
        return jnp.sum(jnp.sum(acc, axis=0, keepdims=True), axis=1, keepdims=True)

    spread = group_sum(0, total_of([a * a for a in advs]))()
    sigma = jnp.sqrt(spread / (group_count * rows * steps * acts) + EPSILON)
    weights = [jnp.exp(jnp.clip(a / sigma, -1.0, 1.0)) for a in advs]
    mass = [jnp.sum(pis[k] * weights[k], axis=0, keepdims=True) for k in range(steps)]
    finish = group_sum(1, total_of(mass))
    scale = 1.0 / (devices * rows * steps)
    g32[...] = jnp.zeros_like(g32)
    partial = []
    for k in range(steps):
        cmpo = pis[k] * weights[k] / mass[k]
        partial.append(pis[k] * jnp.sum(cmpo, axis=0, keepdims=True) - cmpo)
        taken_q = jnp.sum(hots[k] * qs[k], axis=0, keepdims=True)
        g32[k, qrow : qrow + acts, :] = hots[k] * ((taken_q - targets[k]) * scale)
    mean_mass = finish() / (group_count * rows * steps)
    for k in range(steps):
        taken_w = jnp.sum(hots[k] * weights[k], axis=0, keepdims=True) / mean_mass
        g32[k, 0:acts, :] = (partial[k] + taken_w * (pis[k] - hots[k])) * scale
        g_all[:, k * rows : (k + 1) * rows] = g32[k].astype(BF16)

    def head_part(k):
        return dot(g_all[:, k * rows : (k + 1) * rows], whp[...], 0, 0)

    r_ref[...] = head_part(steps - 1)
    for k in range(steps - 2, -1, -1):
        x = (r_ref[...] * deriv[k]).astype(BF16)
        x_all[k * rows : (k + 1) * rows, :] = x
        if k > 0:
            r_ref[...] = r_ref[...] + head_part(k)
            x = x_all[k * rows : (k + 1) * rows, :]
            for at in range(0, hid, 2 * width):
                cols = slice(at, at + 2 * width)
                r_ref[:, cols] = r_ref[:, cols] + dot(wh[cols, :], x, 1, 1).T

    core = bit_value(core_bit)
    other = 1 - core
    used = apad // 8 * 8
    heads_at = hid + used
    ends_at = heads_at + 2 * qrow

    def gradient(owner, color):
        at = pl.multiple_of((owner * COLORS + color) * width, width)
        xb = x_all[:, pl.ds(at, 2 * width)]
        sb = s_all[:, pl.ds(at, 2 * width)]
        gh = dot(s_t[...], xb, 1, 0)
        ga = dot(onehot[:, 0 : (steps - 1) * rows], xb, 1, 0)
        gd = dot(g_all[...], sb, 1, 0)
        for i in range(2):
            slot = owner * COLORS + color + i
            cols = slice(i * width, (i + 1) * width)
            grads[slot, 0:hid, :] = gh[:, cols]
            grads[slot, hid:heads_at, :] = ga[:, cols]
            grads[slot, heads_at:ends_at, :] = gd[:, cols]
            if ends_at < total_rows:
                grads[slot, ends_at:, :] = jnp.zeros((total_rows - ends_at, width), F32)

    mate = partner((core_bit,))
    to_core = []
    for pair in range(0, COLORS, 2):
        gradient(other, pair)
        for color in (pair, pair + 1):
            copy = pltpu.make_async_remote_copy(
                src_ref=grads.at[other * COLORS + color], dst_ref=rcore.at[color],
                send_sem=c1s.at[color], recv_sem=c1r.at[color],
                device_id=mate, device_id_type=MESH,
            )
            copy.start()
            to_core.append(copy)
    for pair in range(0, COLORS, 2):
        gradient(core, pair)

    low = [0] * COLORS
    kept = [[] for _ in range(COLORS)]
    flying = [[] for _ in range(COLORS)]

    def add(color, row, source, src_row, count, target):
        mine = core * COLORS + color
        row = pl.multiple_of(row, 8)
        src_row = pl.multiple_of(src_row, 8)
        target[mine, pl.ds(row, count), :] = (
            grads[mine, pl.ds(row, count), :] + source[color, pl.ds(src_row, count), :]
        )

    offset = 0
    length = total_rows
    for stage in range(stages):
        half = length // 2
        for color in range(COLORS):
            mine = core * COLORS + color
            if stage == 0:
                to_core[color].wait_recv()
                source, base = rcore, 0
            else:
                flying[color][-1].wait_recv()
                source, base = rbuf, offset - length
            v = bit_value(orders[color][stage])
            send, keep = (1 - v) * half, v * half
            add(color, low[color] + send, source, base + send, half, grads)
            copy = pltpu.make_async_remote_copy(
                src_ref=grads.at[mine, pl.ds(pl.multiple_of(low[color] + send, 8), half)],
                dst_ref=rbuf.at[color, pl.ds(offset, half)],
                send_sem=rss.at[color, stage], recv_sem=rsr.at[color, stage],
                device_id=partner((orders[color][stage],)), device_id_type=MESH,
            )
            copy.start()
            flying[color].append(copy)
            add(color, low[color] + keep, source, base + keep, half, grads)
            low[color] = low[color] + keep
            kept[color].append(keep)
        offset += half
        length = half

    to_mate = [[] for _ in range(COLORS)]
    doubling = [[] for _ in range(COLORS)]

    def forward(color, row, count):
        mine = core * COLORS + color
        piece = out.at[mine, pl.ds(pl.multiple_of(row, 8), count)]
        i = len(to_mate[color])
        copy = pltpu.make_async_remote_copy(
            src_ref=piece, dst_ref=piece,
            send_sem=c2s.at[color, i], recv_sem=c2r.at[color, i],
            device_id=mate, device_id_type=MESH,
        )
        copy.start()
        to_mate[color].append(copy)

    def double(color, stage, row, count):
        mine = core * COLORS + color
        piece = out.at[mine, pl.ds(pl.multiple_of(row, 8), count)]
        copy = pltpu.make_async_remote_copy(
            src_ref=piece, dst_ref=piece,
            send_sem=ags.at[color, stage], recv_sem=agr.at[color, stage],
            device_id=partner((orders[color][stage],)), device_id_type=MESH,
        )
        copy.start()
        doubling[color].append(copy)

    for color in range(COLORS):
        flying[color][-1].wait_recv()
        add(color, low[color], rbuf, offset - length, length, out)
        double(color, stages - 1, low[color], length)
        forward(color, low[color], length)
    for stage in range(stages - 1, -1, -1):
        for color in range(COLORS):
            doubling[color][-1].wait_recv()
            keep = kept[color][stage]
            start = low[color] - keep
            if stage > 0:
                double(color, stage - 1, start, 2 * length)
            forward(color, start + length - keep, length)
            low[color] = start
        length *= 2
    for color in range(COLORS):
        for copy in to_mate[color]:
            copy.wait_recv()
    for color in range(COLORS):
        to_core[color].wait_send()
        for copy in flying[color] + doubling[color] + to_mate[color]:
            copy.wait_send()


def layout_kernel(apad, qrow, packed, tgt_in, gh, ga, gd, tgt, sems):
    groups, _, width = packed.shape
    hid = gh.shape[0]
    acts = ga.shape[0]
    copies = []
    for i in range(groups):
        copy = pltpu.make_async_copy(
            packed.at[i, pl.ds(0, hid)], gh.at[:, pl.ds(i * width, width)], sems.at[i]
        )
        copy.start()
        copies.append(copy)
    tgt[...] = tgt_in[...]
    first = hid + apad
    for i in range(groups):
        cols = slice(i * width, (i + 1) * width)
        ga[:, cols] = packed[i, hid : hid + acts, :]
        gd[0:acts, cols] = packed[i, first : first + acts, :]
        gd[acts : 2 * acts, cols] = packed[i, first + qrow : first + qrow + acts, :]
    for copy in copies:
        copy.wait()


def body(plan, embed, actions, rewards, ends, behaviour, w_hidden, w_action, w_heads):
    core_bit, chips, group = plan
    rows, hid = embed.shape
    steps = actions.shape[1]
    acts = w_action.shape[0]
    group_count = lax.axis_size("batch")
    devices = lax.axis_size("rep") * group_count
    orders = color_orders(chips)
    stages = len(orders[0])
    everyone = list(group)
    for bit in [core_bit] + orders[0]:
        if (bit,) not in everyone:
            everyone.append((bit,))
    apad = -(-acts // 16) * 16
    qrow = -(-acts // 32) * 32
    unit = 8 << stages
    total_rows = -(-(hid + apad + 2 * qrow) // unit) * unit
    groups = 2 * COLORS
    width = hid // groups
    cfg = (core_bit, orders, group, everyone, devices, group_count)
    vmem = pl.BlockSpec(memory_space=pltpu.VMEM)
    dma = pltpu.SemaphoreType.DMA
    packed, tgt = pl.pallas_call(
        functools.partial(main_kernel, cfg),
        out_shape=(
            pltpu.VMEM((groups, total_rows, width), F32),
            jax.ShapeDtypeStruct((steps, rows), F32),
        ),
        in_specs=[pl.BlockSpec(memory_space=pltpu.HBM)] * 8,
        out_specs=(vmem, vmem),
        scratch_shapes=[
            pltpu.VMEM((rows, hid), BF16),
            pltpu.VMEM((steps, rows), jnp.int32),
            pltpu.VMEM((steps, rows), F32),
            pltpu.VMEM((steps, rows), jnp.int32),
            pltpu.VMEM((steps, acts, rows), F32),
            pltpu.VMEM((hid, hid), BF16),
            pltpu.VMEM((acts, hid), BF16),
            pltpu.VMEM((2 * acts, hid), BF16),
            dma((8,)),
            pltpu.VMEM((groups, total_rows, width), F32),
            pltpu.VMEM((COLORS, total_rows, width), F32),
            pltpu.VMEM((COLORS, total_rows, width), F32),
            pltpu.VMEM((steps * rows, hid), BF16),
            pltpu.VMEM(((steps - 1) * rows, hid), BF16),
            pltpu.VMEM((hid, (steps - 1) * rows), BF16),
            pltpu.VMEM((steps - 1, rows, hid), F32),
            pltpu.VMEM((rows, hid), F32),
            pltpu.VMEM((rows, hid), F32),
            pltpu.VMEM((2 * qrow, hid), F32),
            pltpu.VMEM((2 * qrow, hid), BF16),
            pltpu.VMEM((apad, hid), BF16),
            pltpu.VMEM((apad, steps * rows), BF16),
            pltpu.VMEM((steps, 2 * qrow, rows), F32),
            pltpu.VMEM((2 * qrow, steps * rows), BF16),
            pltpu.VMEM((2, 8, 128), F32),
            pltpu.VMEM((2, len(group), 8, 128), F32),
            dma((2, len(group))),
            dma((2, len(group))),
            dma((COLORS,)),
            dma((COLORS,)),
            dma((COLORS, stages)),
            dma((COLORS, stages)),
            dma((COLORS, stages)),
            dma((COLORS, stages)),
            dma((COLORS, stages + 1)),
            dma((COLORS, stages + 1)),
        ],
        compiler_params=pltpu.CompilerParams(
            collective_id=0, has_side_effects=True, vmem_limit_bytes=48 * 1024 * 1024
        ),
    )(
        embed, actions.T, rewards.T, ends.T, jnp.transpose(behaviour, (1, 2, 0)),
        w_hidden, w_action, w_heads.T,
    )
    gh, ga, gd, tgt = pl.pallas_call(
        functools.partial(layout_kernel, apad, qrow),
        out_shape=(
            jax.ShapeDtypeStruct((hid, hid), F32),
            jax.ShapeDtypeStruct((acts, hid), F32),
            jax.ShapeDtypeStruct((2 * acts, hid), F32),
            jax.ShapeDtypeStruct((steps, rows), F32),
        ),
        in_specs=[vmem, vmem],
        out_specs=(pl.BlockSpec(memory_space=pl.ANY), vmem, vmem, vmem),
        scratch_shapes=[dma((groups,))],
        compiler_params=pltpu.CompilerParams(vmem_limit_bytes=16 * 1024 * 1024),
    )(packed, tgt)
    return gh, ga, gd.T, tgt.T


def solution(mesh):
    core_bit, chips = topology(mesh)
    batch_bits = []
    stride = 1
    while stride < mesh.shape["batch"]:
        batch_bits.append(("batch", stride))
        stride *= 2
    plan = (core_bit, chips, subsets(batch_bits))
    rows = P(("rep", "batch"), None)
    placed = (rows, rows, rows, rows, P(("rep", "batch"), None, None), P(), P(), P())
    return jax.shard_map(
        functools.partial(body, plan),
        mesh=mesh,
        in_specs=placed,
        out_specs=(P(), P(), P(), rows),
        check_vma=False,
    )
```

```python
import functools

import jax
import jax.numpy as jnp
from jax import lax
from jax.experimental import pallas as pl
from jax.experimental.pallas import tpu as pltpu
from jax.sharding import PartitionSpec as P

DISCOUNT = 0.997
TRACE_LAMBDA = 0.95
EPSILON = 1e-06
MESH = pl.DeviceIdType.MESH
COLORS = 4
PARTS = 3
F32 = jnp.float32
BF16 = jnp.bfloat16


def place_of(device):
    coords = getattr(device, "coords", None)
    if coords is None:
        return None
    return tuple(coords) + (getattr(device, "core_on_chip", 0),)


def topology(mesh):
    devices = mesh.devices
    origin = place_of(devices[(0,) * devices.ndim])
    dims = {}
    for position, axis in enumerate(mesh.axis_names):
        stride = 1
        while stride < devices.shape[position]:
            index = [0] * devices.ndim
            index[position] = stride
            here = place_of(devices[tuple(index)])
            if here is None or origin is None:
                last = position == devices.ndim - 1 and stride == 1
                key, far = ((3,) if last else (0, position, stride)), 1
            else:
                moved = [d for d in range(len(here)) if here[d] != origin[d]]
                key, far = (moved[0],), abs(here[moved[0]] - origin[moved[0]])
            dims.setdefault(key, []).append((far, (axis, stride)))
            stride *= 2
    core = dims.pop((3,))[0][1]
    chips = [[bit for _, bit in sorted(dims[key])] for key in sorted(dims)]
    return core, chips


def color_orders(chips):
    near = [bits[0] for bits in chips]
    rest = [bit for bits in chips for bit in bits[1:]]
    if len(near) == 3:
        turns = ((0, 1, 2), (1, 2, 0), (2, 0, 1))
        perms = [turns[i % PARTS] for i in range(COLORS * PARTS)]
    else:
        n = len(near)
        perms = [[(i + j) % n for j in range(n)] for i in range(COLORS * PARTS)]
    return [[near[i] for i in perm] + rest for perm in perms]


def subsets(bits):
    out = [()]
    for bit in bits:
        out = out + [s + (bit,) for s in out]
    return [s for s in out if s]


def bit_value(bit):
    axis, stride = bit
    return lax.rem(lax.axis_index(axis) // stride, 2)


def partner(bits):
    where = {}
    for axis, stride in bits:
        at = lax.axis_index(axis)
        moved = where.get(axis, at)
        where[axis] = moved + (1 - 2 * lax.rem(at // stride, 2)) * stride
    return where


def dot(a, b, ca, cb):
    return lax.dot_general(a, b, (((ca,), (cb,)), ((), ())), preferred_element_type=F32)


def main_kernel(
    cfg, embed_in, act_in, rew_in, ends_in, beh_in, wh_in, wa_in, wht_in,
    out, tgt, embed, act, rew, ends, beh, wh, wa, wht, in_sem,
    grads, rcore, rbuf, s_all, x_all, s_t, deriv, h_ref, r_ref, whp32, whp, wap, onehot, g32, g_all,
    ssend, srecv,
    ss_sem, sr_sem, c1s, c1r, rss, rsr, ags, agr, c2s, c2r,
):
    core_bit, orders, group, everyone, devices, group_count = cfg
    rows, hid = embed.shape
    steps = act.shape[0]
    acts = wa.shape[0]
    apad = wap.shape[0]
    qrow = whp.shape[0] // 2
    total_rows = grads.shape[1]
    width = grads.shape[2]
    stages = len(orders[0])

    loads = []
    for i, (source, target) in enumerate((
        (embed_in, embed), (act_in, act), (rew_in, rew), (ends_in, ends),
        (beh_in, beh), (wa_in, wa), (wht_in, wht), (wh_in, wh),
    )):
        loads.append(pltpu.make_async_copy(source, target, in_sem.at[i]))
        loads[-1].start()

    barrier = pltpu.get_barrier_semaphore()
    for bits in everyone:
        pl.semaphore_signal(barrier, inc=1, device_id=partner(bits), device_id_type=MESH)

    for load in loads[:-1]:
        load.wait()

    whp32[...] = jnp.zeros_like(whp32)
    whp32[0:acts, :] = wht[0:acts, :].astype(F32)
    whp32[qrow : qrow + acts, :] = wht[acts : 2 * acts, :].astype(F32)
    whp[...] = whp32[...].astype(BF16)
    whp32[...] = jnp.zeros_like(whp32)
    whp32[0:acts, :] = wa[...].astype(F32)
    wap[...] = whp32[0:apad, :].astype(BF16)
    rows_iota = lax.broadcasted_iota(jnp.int32, (apad, rows), 0)
    for k in range(steps):
        hot = rows_iota == act[k : k + 1, :]
        onehot[:, k * rows : (k + 1) * rows] = jnp.where(hot, 1.0, 0.0).astype(BF16)

    loads[-1].wait()
    heads = []
    h_ref[...] = embed[...].astype(F32)
    for k in range(steps + 1):
        s = h_ref[...].astype(BF16)
        if k < steps:
            s_all[k * rows : (k + 1) * rows, :] = s
            pre = dot(s, wh[...], 1, 0) + dot(onehot[:, k * rows : (k + 1) * rows], wap[...], 0, 0)
            t = jnp.tanh(pre)
            h_ref[...] = h_ref[...] + t
            if k < steps - 1:
                deriv[k] = 1.0 - t * t
                s_t[:, k * rows : (k + 1) * rows] = s.T
        heads.append(dot(whp[...], s, 1, 1))

    logits = [o[0:acts] for o in heads]
    qs = [o[qrow : qrow + acts] for o in heads]
    pis, values, logpis, hots, clipped = [], [], [], [], []
    small_iota = lax.broadcasted_iota(jnp.int32, (acts, rows), 0)
    for k in range(steps + 1):
        e = jnp.exp(logits[k])
        z = jnp.sum(e, axis=0, keepdims=True)
        pi = e / z
        pis.append(pi)
        values.append(jnp.sum(pi * qs[k], axis=0, keepdims=True))
        if k < steps:
            logpi = logits[k] - jnp.log(z)
            b = beh[k]
            mu = b - jnp.log(jnp.sum(jnp.exp(b), axis=0, keepdims=True))
            hot = jnp.where(small_iota == act[k : k + 1, :], 1.0, 0.0)
            hots.append(hot)
            ratio = jnp.exp(jnp.sum(hot * (logpi - mu), axis=0, keepdims=True))
            clipped.append(jnp.minimum(1.0, ratio))
    carried = jnp.zeros_like(values[0])
    targets = [None] * steps
    for k in range(steps - 1, -1, -1):
        live = 1.0 - ends[k : k + 1, :].astype(F32)
        delta = rew[k : k + 1, :] + DISCOUNT * live * values[k + 1] - values[k]
        carried = clipped[k] * delta + DISCOUNT * TRACE_LAMBDA * live * clipped[k] * carried
        targets[k] = values[k] + carried
        tgt[k : k + 1, :] = targets[k]
    advs = [qs[k] - values[k] for k in range(steps)]

    pl.semaphore_wait(barrier, len(everyone))

    def group_sum(slot, value):
        ssend[slot] = jnp.broadcast_to(value, ssend.shape[1:])
        copies = [
            pltpu.make_async_remote_copy(
                src_ref=ssend.at[slot], dst_ref=srecv.at[slot, i],
                send_sem=ss_sem.at[slot, i], recv_sem=sr_sem.at[slot, i],
                device_id=partner(bits), device_id_type=MESH,
            )
            for i, bits in enumerate(group)
        ]
        for copy in copies:
            copy.start()

        def finish():
            for copy in copies:
                copy.wait()
            total = ssend[slot]
            for i in range(len(group)):
                total = total + srecv[slot, i]
            return total[0:1, 0:1]

        return finish

    def total_of(parts):
        acc = parts[0]
        for part in parts[1:]:
            acc = acc + part
        return jnp.sum(jnp.sum(acc, axis=0, keepdims=True), axis=1, keepdims=True)

    spread = group_sum(0, total_of([a * a for a in advs]))()
    sigma = jnp.sqrt(spread / (group_count * rows * steps * acts) + EPSILON)
    weights = [jnp.exp(jnp.clip(a / sigma, -1.0, 1.0)) for a in advs]
    mass = [jnp.sum(pis[k] * weights[k], axis=0, keepdims=True) for k in range(steps)]
    finish = group_sum(1, total_of(mass))
    scale = 1.0 / (devices * rows * steps)
    g32[...] = jnp.zeros_like(g32)
    partial = []
    for k in range(steps):
        cmpo = pis[k] * weights[k] / mass[k]
        partial.append(pis[k] * jnp.sum(cmpo, axis=0, keepdims=True) - cmpo)
        taken_q = jnp.sum(hots[k] * qs[k], axis=0, keepdims=True)
        g32[k, qrow : qrow + acts, :] = hots[k] * ((taken_q - targets[k]) * scale)
    mean_mass = finish() / (group_count * rows * steps)
    for k in range(steps):
        taken_w = jnp.sum(hots[k] * weights[k], axis=0, keepdims=True) / mean_mass
        g32[k, 0:acts, :] = (partial[k] + taken_w * (pis[k] - hots[k])) * scale
        g_all[:, k * rows : (k + 1) * rows] = g32[k].astype(BF16)

    def head_part(k):
        return dot(g_all[:, k * rows : (k + 1) * rows], whp[...], 0, 0)

    r_ref[...] = head_part(steps - 1)
    for k in range(steps - 2, -1, -1):
        x = (r_ref[...] * deriv[k]).astype(BF16)
        x_all[k * rows : (k + 1) * rows, :] = x
        if k > 0:
            r_ref[...] = r_ref[...] + head_part(k)
            x = x_all[k * rows : (k + 1) * rows, :]
            for at in range(0, hid, 2 * width):
                cols = slice(at, at + 2 * width)
                r_ref[:, cols] = r_ref[:, cols] + dot(wh[cols, :], x, 1, 1).T

    core = bit_value(core_bit)
    other = 1 - core
    used = apad // 8 * 8
    heads_at = hid + used
    ends_at = heads_at + 2 * qrow

    def gradient(owner, color):
        at = pl.multiple_of((owner * COLORS + color) * width, width)
        xb = x_all[:, pl.ds(at, 2 * width)]
        sb = s_all[:, pl.ds(at, 2 * width)]
        gh = dot(s_t[...], xb, 1, 0)
        ga = dot(onehot[:, 0 : (steps - 1) * rows], xb, 1, 0)
        gd = dot(g_all[...], sb, 1, 0)
        for i in range(2):
            slot = owner * COLORS + color + i
            cols = slice(i * width, (i + 1) * width)
            grads[slot, 0:hid, :] = gh[:, cols]
            grads[slot, hid:heads_at, :] = ga[:, cols]
            grads[slot, heads_at:ends_at, :] = gd[:, cols]
            if ends_at < total_rows:
                grads[slot, ends_at:, :] = jnp.zeros((total_rows - ends_at, width), F32)

    mate = partner((core_bit,))
    to_core = []
    for pair in range(0, COLORS, 2):
        gradient(other, pair)
        for color in (pair, pair + 1):
            copy = pltpu.make_async_remote_copy(
                src_ref=grads.at[other * COLORS + color], dst_ref=rcore.at[color],
                send_sem=c1s.at[color], recv_sem=c1r.at[color],
                device_id=mate, device_id_type=MESH,
            )
            copy.start()
            to_core.append(copy)
    for pair in range(0, COLORS, 2):
        gradient(core, pair)

    chains = COLORS * PARTS
    part = total_rows // PARTS
    first = [(c % PARTS) * part for c in range(chains)]
    low = list(first)
    kept = [[] for _ in range(chains)]
    flying = [[] for _ in range(chains)]

    def add(chain, row, source, src_row, count, target):
        color = chain // PARTS
        mine = core * COLORS + color
        row = pl.multiple_of(row, 8)
        src_row = pl.multiple_of(src_row, 8)
        target[mine, pl.ds(row, count), :] = (
            grads[mine, pl.ds(row, count), :] + source[color, pl.ds(src_row, count), :]
        )

    offset = 0
    length = part
    for stage in range(stages):
        half = length // 2
        for chain in range(chains):
            color = chain // PARTS
            mine = core * COLORS + color
            if stage == 0:
                if chain % PARTS == 0:
                    to_core[color].wait_recv()
                source, base = rcore, first[chain]
            else:
                flying[chain][-1].wait_recv()
                source, base = rbuf, first[chain] + offset - length
            v = bit_value(orders[chain][stage])
            send, keep = (1 - v) * half, v * half
            add(chain, low[chain] + send, source, base + send, half, grads)
            copy = pltpu.make_async_remote_copy(
                src_ref=grads.at[mine, pl.ds(pl.multiple_of(low[chain] + send, 8), half)],
                dst_ref=rbuf.at[color, pl.ds(first[chain] + offset, half)],
                send_sem=rss.at[chain, stage], recv_sem=rsr.at[chain, stage],
                device_id=partner((orders[chain][stage],)), device_id_type=MESH,
            )
            copy.start()
            flying[chain].append(copy)
            add(chain, low[chain] + keep, source, base + keep, half, grads)
            low[chain] = low[chain] + keep
            kept[chain].append(keep)
        offset += half
        length = half

    to_mate = [[] for _ in range(chains)]
    doubling = [[] for _ in range(chains)]

    def forward(chain, row, count):
        mine = core * COLORS + chain // PARTS
        piece = out.at[mine, pl.ds(pl.multiple_of(row, 8), count)]
        i = len(to_mate[chain])
        copy = pltpu.make_async_remote_copy(
            src_ref=piece, dst_ref=piece,
            send_sem=c2s.at[chain, i], recv_sem=c2r.at[chain, i],
            device_id=mate, device_id_type=MESH,
        )
        copy.start()
        to_mate[chain].append(copy)

    def double(chain, stage, row, count):
        mine = core * COLORS + chain // PARTS
        piece = out.at[mine, pl.ds(pl.multiple_of(row, 8), count)]
        copy = pltpu.make_async_remote_copy(
            src_ref=piece, dst_ref=piece,
            send_sem=ags.at[chain, stage], recv_sem=agr.at[chain, stage],
            device_id=partner((orders[chain][stage],)), device_id_type=MESH,
        )
        copy.start()
        doubling[chain].append(copy)

    for chain in range(chains):
        flying[chain][-1].wait_recv()
        add(chain, low[chain], rbuf, first[chain] + offset - length, length, out)
        double(chain, stages - 1, low[chain], length)
        forward(chain, low[chain], length)
    for stage in range(stages - 1, -1, -1):
        for chain in range(chains):
            doubling[chain][-1].wait_recv()
            keep = kept[chain][stage]
            start = low[chain] - keep
            if stage > 0:
                double(chain, stage - 1, start, 2 * length)
            forward(chain, start + length - keep, length)
            low[chain] = start
        length *= 2
    for chain in range(chains):
        for copy in to_mate[chain]:
            copy.wait_recv()
    for color in range(COLORS):
        to_core[color].wait_send()
    for chain in range(chains):
        for copy in flying[chain] + doubling[chain] + to_mate[chain]:
            copy.wait_send()


def layout_kernel(apad, qrow, packed, tgt_in, gh, ga, gd, tgt, sems):
    groups, _, width = packed.shape
    hid = gh.shape[0]
    acts = ga.shape[0]
    copies = []
    for i in range(groups):
        copy = pltpu.make_async_copy(
            packed.at[i, pl.ds(0, hid)], gh.at[:, pl.ds(i * width, width)], sems.at[i]
        )
        copy.start()
        copies.append(copy)
    tgt[...] = tgt_in[...]
    first = hid + apad
    for i in range(groups):
        cols = slice(i * width, (i + 1) * width)
        ga[:, cols] = packed[i, hid : hid + acts, :]
        gd[0:acts, cols] = packed[i, first : first + acts, :]
        gd[acts : 2 * acts, cols] = packed[i, first + qrow : first + qrow + acts, :]
    for copy in copies:
        copy.wait()


def body(plan, embed, actions, rewards, ends, behaviour, w_hidden, w_action, w_heads):
    core_bit, chips, group = plan
    rows, hid = embed.shape
    steps = actions.shape[1]
    acts = w_action.shape[0]
    group_count = lax.axis_size("batch")
    devices = lax.axis_size("rep") * group_count
    orders = color_orders(chips)
    stages = len(orders[0])
    everyone = list(group)
    for bit in [core_bit] + orders[0]:
        if (bit,) not in everyone:
            everyone.append((bit,))
    apad = -(-acts // 16) * 16
    qrow = -(-acts // 32) * 32
    unit = PARTS * 8 << stages
    total_rows = -(-(hid + apad + 2 * qrow) // unit) * unit
    groups = 2 * COLORS
    width = hid // groups
    cfg = (core_bit, orders, group, everyone, devices, group_count)
    vmem = pl.BlockSpec(memory_space=pltpu.VMEM)
    dma = pltpu.SemaphoreType.DMA
    packed, tgt = pl.pallas_call(
        functools.partial(main_kernel, cfg),
        out_shape=(
            pltpu.VMEM((groups, total_rows, width), F32),
            jax.ShapeDtypeStruct((steps, rows), F32),
        ),
        in_specs=[pl.BlockSpec(memory_space=pltpu.HBM)] * 8,
        out_specs=(vmem, vmem),
        scratch_shapes=[
            pltpu.VMEM((rows, hid), BF16),
            pltpu.VMEM((steps, rows), jnp.int32),
            pltpu.VMEM((steps, rows), F32),
            pltpu.VMEM((steps, rows), jnp.int32),
            pltpu.VMEM((steps, acts, rows), F32),
            pltpu.VMEM((hid, hid), BF16),
            pltpu.VMEM((acts, hid), BF16),
            pltpu.VMEM((2 * acts, hid), BF16),
            dma((8,)),
            pltpu.VMEM((groups, total_rows, width), F32),
            pltpu.VMEM((COLORS, total_rows, width), F32),
            pltpu.VMEM((COLORS, total_rows, width), F32),
            pltpu.VMEM((steps * rows, hid), BF16),
            pltpu.VMEM(((steps - 1) * rows, hid), BF16),
            pltpu.VMEM((hid, (steps - 1) * rows), BF16),
            pltpu.VMEM((steps - 1, rows, hid), F32),
            pltpu.VMEM((rows, hid), F32),
            pltpu.VMEM((rows, hid), F32),
            pltpu.VMEM((2 * qrow, hid), F32),
            pltpu.VMEM((2 * qrow, hid), BF16),
            pltpu.VMEM((apad, hid), BF16),
            pltpu.VMEM((apad, steps * rows), BF16),
            pltpu.VMEM((steps, 2 * qrow, rows), F32),
            pltpu.VMEM((2 * qrow, steps * rows), BF16),
            pltpu.VMEM((2, 8, 128), F32),
            pltpu.VMEM((2, len(group), 8, 128), F32),
            dma((2, len(group))),
            dma((2, len(group))),
            dma((COLORS,)),
            dma((COLORS,)),
            dma((COLORS * PARTS, stages)),
            dma((COLORS * PARTS, stages)),
            dma((COLORS * PARTS, stages)),
            dma((COLORS * PARTS, stages)),
            dma((COLORS * PARTS, stages + 1)),
            dma((COLORS * PARTS, stages + 1)),
        ],
        compiler_params=pltpu.CompilerParams(
            collective_id=0, has_side_effects=True, vmem_limit_bytes=48 * 1024 * 1024
        ),
    )(
        embed, actions.T, rewards.T, ends.T, jnp.transpose(behaviour, (1, 2, 0)),
        w_hidden, w_action, w_heads.T,
    )
    gh, ga, gd, tgt = pl.pallas_call(
        functools.partial(layout_kernel, apad, qrow),
        out_shape=(
            jax.ShapeDtypeStruct((hid, hid), F32),
            jax.ShapeDtypeStruct((acts, hid), F32),
            jax.ShapeDtypeStruct((2 * acts, hid), F32),
            jax.ShapeDtypeStruct((steps, rows), F32),
        ),
        in_specs=[vmem, vmem],
        out_specs=(pl.BlockSpec(memory_space=pl.ANY), vmem, vmem, vmem),
        scratch_shapes=[dma((groups,))],
        compiler_params=pltpu.CompilerParams(vmem_limit_bytes=16 * 1024 * 1024),
    )(packed, tgt)
    return gh, ga, gd.T, tgt.T


def solution(mesh):
    core_bit, chips = topology(mesh)
    batch_bits = []
    stride = 1
    while stride < mesh.shape["batch"]:
        batch_bits.append(("batch", stride))
        stride *= 2
    plan = (core_bit, chips, subsets(batch_bits))
    rows = P(("rep", "batch"), None)
    placed = (rows, rows, rows, rows, P(("rep", "batch"), None, None), P(), P(), P())
    return jax.shard_map(
        functools.partial(body, plan),
        mesh=mesh,
        in_specs=placed,
        out_specs=(P(), P(), P(), rows),
        check_vma=False,
    )
```
